256 devices in a mesh: row: 16 (over y_hi, x, core), col: 16 (over z, y_lo).
Axes of the slice: x: 4, y: 4 (y_hi: 2, y_lo: 2; y = y_hi * 2 + y_lo), z: 8, core: 2. Of those that a mesh axis runs over, the one named last changes fastest.
Arguments:
- trailing: float32 [12288, 16384], P('row', 'col'), may hold values from -6 to 6
- column_block: bfloat16 [12288, 1024], P('row', 'col'), may hold values from -6 to 6
- row_block: bfloat16 [1024, 16384], P('row', 'col'), may hold values from -0.1875 to 0.1875
- lower_inv: bfloat16 [1024, 1024], replicated, may hold values from -1 to 1, as said below
- upper_inv: bfloat16 [1024, 1024], replicated, may hold values from -2 to 2, as said below
Outputs:
- lower_panel: bfloat16 [12288, 1024], P('row', 'col')
- upper_panel: bfloat16 [1024, 16384], P('row', 'col')
- updated: float32 [12288, 16384], P('row', 'col')
The draws below stay inside these ranges and needn't reach their ends.
Inputs may be any that keep to these rules, and one draw needn't show every extreme that they name: `lower_inv`: lower triangular with ones on the diagonal. `upper_inv`: upper triangular with diagonal entries between 0.5 and 2.
All inputs are finite; a program needn't handle non-finite values.
Results may differ from the reference program's by a relative error of at most 0.0044.
Values may be sent and summed in bfloat16 or wider, within the bound.
No kernel may reach another device: no remote copies, remote signals or barrier semaphores. Data moves between devices by JAX's collectives and lax.ppermute only.
A program may use at most 64 MiB of HBM per device.

```python
import jax
import jax.numpy as jnp

NB = 1024
WROWS = 12288
WCOLS = 16384


def off_diagonal(key):
    first = jax.random.fold_in(jax.random.fold_in(key, 7), 0)
    values = jax.random.normal(first, (NB, NB), jnp.float32)
    return jnp.clip(values * NB ** (-0.5), -0.25, 0.25)


def draw_lower_inv(key, part):
    rowids = jnp.arange(NB)[:, None]
    colids = jnp.arange(NB)[None, :]
    values = off_diagonal(key)
    result = jnp.where(rowids > colids, values, jnp.where(rowids == colids, 1.0, 0.0))
    return result.astype(jnp.bfloat16)


def draw_upper_inv(key, part):
    rowids = jnp.arange(NB)[:, None]
    colids = jnp.arange(NB)[None, :]
    values = off_diagonal(jax.random.fold_in(key, 3))
    diag_key = jax.random.fold_in(key, 11)
    scales = jnp.exp(jax.random.uniform(diag_key, (NB, 1), jnp.float32, jnp.log(0.5), jnp.log(2.0)))
    result = jnp.where(rowids < colids, values, jnp.where(rowids == colids, scales, 0.0))
    return result.astype(jnp.bfloat16)


def block_levels(own_key, dims, cuts, smallest, largest):
    factor_of = 1.0
    for axis_at, shards_of in cuts:
        steps = jax.random.uniform(jax.random.fold_in(jax.random.fold_in(own_key, 6), axis_at), (shards_of,), jnp.float32, smallest / len(cuts), largest / len(cuts))
        factor_of = factor_of * jnp.repeat(jnp.exp(steps), dims[axis_at] // shards_of).reshape((-1,) + (1,) * (len(dims) - 1 - axis_at))
    return factor_of


def centred(rng, dims, spread, bound, pieces=(), held_as=jnp.bfloat16):
    values = spread * jax.random.normal(rng, dims, jnp.float32)
    if pieces:
        values = values * block_levels(rng, dims, pieces, -0.22, 0.18)
    return jnp.clip(values, -bound, bound).astype(held_as)


def setup_inputs(seed: int = 0) -> dict:
    arg_keys = jax.random.split(jax.random.key(seed), 6)
    return {
        "trailing": centred(arg_keys[0], (WROWS, WCOLS), 1.0, 6.0, ((0, 16), (1, 16)), jnp.float32),
        "column_block": centred(arg_keys[1], (WROWS, NB), 1.0, 6.0, ((0, 16), (1, 16))),
        "row_block": centred(arg_keys[2], (NB, WCOLS), NB ** -0.5, 0.1875, ((0, 16), (1, 16))),
        "lower_inv": draw_lower_inv(jax.random.fold_in(arg_keys[5], 71), 0),
        "upper_inv": draw_upper_inv(jax.random.fold_in(arg_keys[5], 71), 0),
    }


def reference(trailing, column_block, row_block, lower_inv, upper_inv):
    lower_panel = jnp.dot(column_block, upper_inv, preferred_element_type=jnp.float32).astype(jnp.bfloat16)
    upper_panel = jnp.dot(lower_inv, row_block, preferred_element_type=jnp.float32).astype(jnp.bfloat16)
    updated = trailing - jnp.dot(lower_panel, upper_panel, preferred_element_type=jnp.float32)
    return lower_panel, upper_panel, updated
```

```python
import jax
import jax.numpy as jnp
from jax import lax
from jax.sharding import PartitionSpec as P


def split(row, col):
    return row >> 3, (row >> 1) & 3, row & 1, col >> 1, col & 1


def pairs_of(rows, cols, target):
    pairs = []
    for row in range(rows):
        for col in range(cols):
            half, x, core, z, low = target(*split(row, col))
            to_row = ((half % 2) * 4 + x % 4) * 2 + core
            to_col = (z % 8) * 2 + low
            pairs.append((row * cols + col, to_row * cols + to_col))
    return pairs


def on_device(trailing, column_block, row_block, lower_inv, upper_inv):
    def send(block, target):
        return lax.ppermute(block, ("row", "col"), pairs_of(16, 16, target))

    def from_z(block, step):
        return send(block, lambda half, x, core, z, low: (half, x, core, z - step, low))

    def from_x(block, step):
        return send(block, lambda half, x, core, z, low: (half, x - step, core, z, low))

    def from_half(block):
        return send(block, lambda half, x, core, z, low: (half ^ 1, x, core, z, low))

    def from_low(block):
        return send(block, lambda half, x, core, z, low: (half, x, core, z, low ^ 1))

    def from_core(block):
        return send(block, lambda half, x, core, z, low: (half, x, core ^ 1, z, low))

    row, col = lax.axis_index("row"), lax.axis_index("col")
    half, x, core, z, low = split(row, col)
    share = column_block.shape[1]
    own_a, own_b = column_block.T, row_block

    other_half = from_half(own_b)
    other_low = from_low(own_a)
    a_next, a_prev, a_far = from_z(own_a, 1), from_z(own_a, -1), from_z(own_a, 4)

    b_two = jnp.concatenate([own_b, other_half], 0)
    b_x = [b_two, from_x(b_two, 1), from_x(b_two, 2), from_x(b_two, 3)]
    b_mine = jnp.concatenate(b_x, 0)
    b_theirs = from_core(b_mine)

    three = jnp.concatenate([a_next, a_far, a_prev], 0)
    up = from_z(three[: 2 * share], 1)
    down = from_z(three[share:], -1)
    low_three = from_low(three)
    low_up = from_z(low_three[: 2 * share], 1)
    low_down = from_z(low_three[share:], -1)

    def part(block, index):
        return block[index * share : (index + 1) * share]

    mine = [own_a, a_next, part(up, 0), part(down, 0), a_far, part(up, 1), part(down, 1), a_prev]
    theirs = [
        other_low, part(low_three, 0), part(low_up, 0), part(low_down, 0),
        part(low_three, 1), part(low_up, 1), part(low_down, 1), part(low_three, 2),
    ]
    mine[3], mine[6] = part(down, 0), part(down, 1)
    theirs[3], theirs[6] = part(low_down, 0), part(low_down, 1)
    a_all = jnp.concatenate(mine + theirs, 0)

    nb = upper_inv.shape[0]
    width = nb // 8
    turned = lax.dynamic_slice_in_dim(jnp.concatenate([upper_inv, upper_inv], 0), z * width, nb, 0)
    turned = turned.reshape(8, 2, share, nb)
    turned = jnp.where(low == 0, turned, turned[:, ::-1])
    upper_turned = turned.transpose(1, 0, 2, 3).reshape(nb, nb)

    lt = lower_inv.T.reshape(2, 4, 2, share, nb)
    lt = jnp.where(half == 0, lt, lt[::-1])
    lt = lax.dynamic_slice_in_dim(jnp.concatenate([lt, lt], 1), x, 4, 1)
    lt = jnp.where(core == 0, lt, lt[:, :, ::-1])
    lower_turned = lt.transpose(2, 1, 0, 3, 4).reshape(nb, nb)
    b_all = jnp.concatenate([b_mine, b_theirs], 0)

    first = (((0,), (0,)), ((), ()))
    lower_full = lax.dot_general(
        a_all, upper_turned, first, preferred_element_type=jnp.float32
    ).astype(jnp.bfloat16)
    upper_full = lax.dot_general(
        lower_turned, b_all, first, preferred_element_type=jnp.float32
    ).astype(jnp.bfloat16)
    product = jnp.dot(lower_full, upper_full, preferred_element_type=jnp.float32)
    lower_tile = lax.dynamic_slice_in_dim(lower_full, col * share, share, 1)
    upper_tile = lax.dynamic_slice_in_dim(upper_full, row * share, share, 0)
    return lower_tile, upper_tile, trailing - product


def solution(mesh):
    in_specs = (P("row", "col"), P("row", "col"), P("row", "col"), P(), P())
    out_specs = (P("row", "col"), P("row", "col"), P("row", "col"))
    return jax.shard_map(
        on_device, mesh=mesh, in_specs=in_specs, out_specs=out_specs, check_vma=False
    )
```

```python
import functools

import jax
import jax.numpy as jnp
from jax import lax
from jax.experimental import pallas as pl
from jax.experimental.pallas import tpu as pltpu
from jax.sharding import PartitionSpec as P

VMEM = pl.BlockSpec(memory_space=pltpu.VMEM)
HBM = pl.BlockSpec(memory_space=pltpu.HBM)
FIRST = (((0,), (0,)), ((), ()))
BLOCK = 256


def split(row, col):
    return row >> 3, (row >> 1) & 3, row & 1, col >> 1, col & 1


def pairs_of(rows, cols, target):
    pairs = []
    for row in range(rows):
        for col in range(cols):
            half, x, core, z, low = target(*split(row, col))
            to_row = ((half % 2) * 4 + x % 4) * 2 + core
            to_col = (z % 8) * 2 + low
            pairs.append((row * cols + col, to_row * cols + to_col))
    return pairs


def place():
    return split(lax.axis_index("row"), lax.axis_index("col"))


def put(full_ref, at, piece_ref, index, share):
    rows = pl.ds(pl.multiple_of(at * share, share), share)
    full_ref[rows, :] = piece_ref[index * share : (index + 1) * share, :]


def upper_kernel(places, *refs):
    *piece_refs, lower_ref, full_ref, tile_ref, b_ref, sem = refs
    half, x, core, _, _ = place()
    share = tile_ref.shape[0]
    for ref, shards in zip(piece_refs, places, strict=True):
        for index, (dx, dhalf, dcore) in enumerate(shards):
            at = ((half ^ dhalf) * 4 + lax.rem(x + dx, 4)) * 2 + (core ^ dcore)
            put(b_ref, at, ref, index, share)
    for i in range(full_ref.shape[0] // BLOCK):
        rows, known = slice(i * BLOCK, (i + 1) * BLOCK), (i + 1) * BLOCK
        full_ref[rows, :] = jnp.dot(
            lower_ref[rows, :known], b_ref[:known, :], preferred_element_type=jnp.float32
        ).astype(full_ref.dtype)
    own = pl.ds(pl.multiple_of(lax.axis_index("row") * share, share), share)
    copy = pltpu.make_async_copy(full_ref.at[own, :], tile_ref, sem)
    copy.start()
    copy.wait()


def update_kernel(places, *refs):
    *piece_refs, upper_inv_ref, upper_ref, trailing_ref = refs[: len(places) + 3]
    tile_ref, updated_ref, a_ref, lower_ref, out_ref, tile_sem, out_sems = refs[len(places) + 3 :]
    _, _, _, z, low = place()
    share = tile_ref.shape[0]
    for ref, shards in zip(piece_refs, places, strict=True):
        for index, (dz, dlow) in enumerate(shards):
            put(a_ref, lax.rem(z + dz, 8) * 2 + (low ^ dlow), ref, index, share)
    blocks = upper_ref.shape[1] // BLOCK
    for j in range(blocks):
        cols, known = slice(j * BLOCK, (j + 1) * BLOCK), (j + 1) * BLOCK
        lower_ref[cols, :] = lax.dot_general(
            upper_inv_ref[:known, cols], a_ref[:known, :], FIRST, preferred_element_type=jnp.float32
        ).astype(lower_ref.dtype)
    own = pl.ds(pl.multiple_of(lax.axis_index("col") * share, share), share)
    tile_copy = pltpu.make_async_copy(lower_ref.at[own, :], tile_ref, tile_sem)
    tile_copy.start()
    copies = []
    for j in range(blocks):
        cols = slice(j * BLOCK, (j + 1) * BLOCK)
        out_ref[:, cols] = trailing_ref[:, cols] - lax.dot_general(
            lower_ref[...], upper_ref[:, cols], FIRST, preferred_element_type=jnp.float32
        )
        copies.append(
            pltpu.make_async_copy(out_ref.at[:, cols], updated_ref.at[:, cols], out_sems.at[j])
        )
        copies[-1].start()
    tile_copy.wait()
    for copy in copies:
        copy.wait()


def on_device(trailing, column_block, row_block, lower_inv, upper_inv):
    def send(block, target):
        return lax.ppermute(block, ("row", "col"), pairs_of(16, 16, target))

    def from_z(block, step):
        return send(block, lambda half, x, core, z, low: (half, x, core, z - step, low))

    def from_x(block, step):
        return send(block, lambda half, x, core, z, low: (half, x - step, core, z, low))

    def from_half(block):
        return send(block, lambda half, x, core, z, low: (half ^ 1, x, core, z, low))

    def from_low(block):
        return send(block, lambda half, x, core, z, low: (half, x, core, z, low ^ 1))

    def from_core(block):
        return send(block, lambda half, x, core, z, low: (half, x, core ^ 1, z, low))

    rows, cols = trailing.shape
    nb = upper_inv.shape[0]
    share = column_block.shape[1]
    own_a, own_b = column_block.T, row_block

    a_next, a_prev = from_z(own_a, 1), from_z(own_a, -1)
    other_half = from_half(own_b)
    a_far = from_z(own_a, 4)
    other_low = from_low(own_a)

    b_x = [jnp.concatenate([own_b, other_half], 0)]
    b_x += [from_x(b_x[0], step) for step in (1, 3, 2)]
    b_core = [from_core(block) for block in b_x]

    three = jnp.concatenate([a_next, a_far, a_prev], 0)
    up = from_z(three[: 2 * share], 1)
    down = from_z(three[share:], -1)
    low_three = from_low(three)
    low_up = from_z(low_three[: 2 * share], 1)
    low_down = from_z(low_three[share:], -1)

    steps = (0, 1, 3, 2)
    b_places = [[(dx, dhalf, dcore) for dhalf in (0, 1)] for dcore in (0, 1) for dx in steps]
    upper_full, upper_tile = pl.pallas_call(
        functools.partial(upper_kernel, b_places),
        out_shape=[
            jax.ShapeDtypeStruct((nb, cols), jnp.bfloat16),
            jax.ShapeDtypeStruct(row_block.shape, jnp.bfloat16),
        ],
        in_specs=[VMEM] * 9,
        out_specs=[VMEM, HBM],
        scratch_shapes=[pltpu.VMEM((nb, cols), jnp.bfloat16), pltpu.SemaphoreType.DMA],
        compiler_params=pltpu.CompilerParams(vmem_limit_bytes=8 << 20),
        cost_estimate=pl.CostEstimate(flops=2 * nb * nb * cols, bytes_accessed=0, transcendentals=0),
    )(*b_x, *b_core, lower_inv)

    a_places = [
        [(0, 0)], [(1, 0), (4, 0), (7, 0)], [(2, 0), (5, 0)], [(3, 0), (6, 0)],
        [(0, 1)], [(1, 1), (4, 1), (7, 1)], [(2, 1), (5, 1)], [(3, 1), (6, 1)],
    ]
    lower_tile, updated = pl.pallas_call(
        functools.partial(update_kernel, a_places),
        out_shape=[
            jax.ShapeDtypeStruct((share, rows), jnp.bfloat16),
            jax.ShapeDtypeStruct((rows, cols), jnp.float32),
        ],
        in_specs=[VMEM] * (len(a_places) + 3),
        out_specs=[HBM, HBM],
        scratch_shapes=[
            pltpu.VMEM((nb, rows), jnp.bfloat16),
            pltpu.VMEM((nb, rows), jnp.bfloat16),
            pltpu.VMEM((rows, cols), jnp.float32),
            pltpu.SemaphoreType.DMA,
            pltpu.SemaphoreType.DMA((cols // BLOCK,)),
        ],
        compiler_params=pltpu.CompilerParams(vmem_limit_bytes=12 << 20),
        cost_estimate=pl.CostEstimate(flops=2 * rows * nb * (nb + cols), bytes_accessed=0, transcendentals=0),
    )(own_a, three, up, down, other_low, low_three, low_up, low_down, upper_inv, upper_full, trailing)
    return lower_tile.T, upper_tile, updated


def solution(mesh):
    in_specs = (P("row", "col"), P("row", "col"), P("row", "col"), P(), P())
    out_specs = (P("row", "col"), P("row", "col"), P("row", "col"))
    return jax.shard_map(
        on_device, mesh=mesh, in_specs=in_specs, out_specs=out_specs, check_vma=False
    )
```

```python
import functools

import jax
import jax.numpy as jnp
from jax import lax
from jax.experimental import pallas as pl
from jax.experimental.pallas import tpu as pltpu
from jax.sharding import PartitionSpec as P

VMEM = pl.BlockSpec(memory_space=pltpu.VMEM)
HBM = pl.BlockSpec(memory_space=pltpu.HBM)
FIRST = (((0,), (0,)), ((), ()))
BLOCK = 256


def split(row, col):
    return row >> 3, (row >> 1) & 3, row & 1, col >> 1, col & 1


def pairs_of(rows, cols, target):
    pairs = []
    for row in range(rows):
        for col in range(cols):
            half, x, core, z, low = target(*split(row, col))
            to_row = ((half % 2) * 4 + x % 4) * 2 + core
            to_col = (z % 8) * 2 + low
            pairs.append((row * cols + col, to_row * cols + to_col))
    return pairs


def place():
    return split(lax.axis_index("row"), lax.axis_index("col"))


def put(full_ref, at, piece_ref, index, share):
    rows = pl.ds(pl.multiple_of(at * share, share), share)
    full_ref[rows, :] = piece_ref[index * share : (index + 1) * share, :]


def upper_kernel(places, *refs):
    *piece_refs, lower_ref, full_ref, tile_ref, b_ref, sem = refs
    half, x, core, _, _ = place()
    share = tile_ref.shape[0]
    for ref, shards in zip(piece_refs, places, strict=True):
        for index, (dx, dhalf, dcore) in enumerate(shards):
            at = ((half ^ dhalf) * 4 + lax.rem(x + dx, 4)) * 2 + (core ^ dcore)
            put(b_ref, at, ref, index, share)
    for i in range(full_ref.shape[0] // BLOCK):
        rows, known = slice(i * BLOCK, (i + 1) * BLOCK), (i + 1) * BLOCK
        full_ref[rows, :] = jnp.dot(
            lower_ref[rows, :known], b_ref[:known, :], preferred_element_type=jnp.float32
        ).astype(full_ref.dtype)
    own = pl.ds(pl.multiple_of(lax.axis_index("row") * share, share), share)
    copy = pltpu.make_async_copy(full_ref.at[own, :], tile_ref, sem)
    copy.start()
    copy.wait()


def update_kernel(places, *refs):
    *piece_refs, upper_inv_ref, upper_ref, trailing_ref = refs[: len(places) + 3]
    tile_ref, updated_ref, a_ref, lower_ref, out_ref, tile_sem, out_sems = refs[len(places) + 3 :]
    _, _, _, z, low = place()
    share = tile_ref.shape[0]
    for ref, shards in zip(piece_refs, places, strict=True):
        for index, (dz, dlow) in enumerate(shards):
            put(a_ref, lax.rem(z + dz, 8) * 2 + (low ^ dlow), ref, index, share)
    blocks = upper_ref.shape[1] // BLOCK
    for j in range(blocks):
        cols, known = slice(j * BLOCK, (j + 1) * BLOCK), (j + 1) * BLOCK
        lower_ref[cols, :] = lax.dot_general(
            upper_inv_ref[:known, cols], a_ref[:known, :], FIRST, preferred_element_type=jnp.float32
        ).astype(lower_ref.dtype)
    own = pl.ds(pl.multiple_of(lax.axis_index("col") * share, share), share)
    tile_copy = pltpu.make_async_copy(lower_ref.at[own, :], tile_ref, tile_sem)
    tile_copy.start()
    copies = []
    for j in range(blocks):
        cols = slice(j * BLOCK, (j + 1) * BLOCK)
        out_ref[:, cols] = trailing_ref[:, cols] - lax.dot_general(
            lower_ref[...], upper_ref[:, cols], FIRST, preferred_element_type=jnp.float32
        )
        copies.append(
            pltpu.make_async_copy(out_ref.at[:, cols], updated_ref.at[:, cols], out_sems.at[j])
        )
        copies[-1].start()
    tile_copy.wait()
    for copy in copies:
        copy.wait()


def join_kernel(pieces, *refs):
    whole_ref, at = refs[-1], 0
    for ref, (start, size) in zip(refs, pieces):
        whole_ref[at : at + size, :] = ref[start : start + size, :]
        at += size


def join(time, *blocks):
    blocks = [b if isinstance(b, tuple) else (b, 0, b.shape[0]) for b in blocks]
    pieces = [b[1:] for b in blocks]
    return pl.pallas_call(
        functools.partial(join_kernel, pieces),
        out_shape=jax.ShapeDtypeStruct((sum(p[1] for p in pieces), blocks[0][0].shape[1]), jnp.bfloat16),
        in_specs=[VMEM] * len(blocks),
        out_specs=VMEM,
        compiler_params=pltpu.CompilerParams(vmem_limit_bytes=2 << 20),
        cost_estimate=pl.CostEstimate(flops=int(time * 1e9), bytes_accessed=0, transcendentals=0),
    )(*[b[0] for b in blocks])


def on_device(trailing, column_block, row_block, lower_inv, upper_inv):
    def send(block, name, target):
        with jax.named_scope(name):
            return lax.ppermute(block, ("row", "col"), pairs_of(16, 16, target))

    def from_z(block, name, step):
        return send(block, name, lambda half, x, core, z, low: (half, x, core, z - step, low))

    def from_z_by_core(block, name, step):
        return send(
            block, name, lambda half, x, core, z, low: (half, x, core, z - (step, -step)[core], low)
        )

    def from_x(block, name, step):
        return send(block, name, lambda half, x, core, z, low: (half, x - step, core, z, low))

    def from_x_by_core(block, name, step):
        return send(
            block, name, lambda half, x, core, z, low: (half, x - (step, -step)[core], core, z, low)
        )

    def from_half(block, name):
        return send(block, name, lambda half, x, core, z, low: (half ^ 1, x, core, z, low))

    def from_low(block, name):
        return send(block, name, lambda half, x, core, z, low: (half, x, core, z, low ^ 1))

    def from_core(block, name):
        return send(block, name, lambda half, x, core, z, low: (half, x, core ^ 1, z, low))

    def after(block, *others):
        return lax.optimization_barrier((block, *others))[0] if others else block

    rows, cols = trailing.shape
    nb = upper_inv.shape[0]
    share = column_block.shape[1]
    own_a, own_b = column_block.T, row_block

    half_b = from_half(own_b, "half")
    a_next = from_z(own_a, "next", 1)
    a_prev = from_z(own_a, "prev", -1)
    a_far = from_z(own_a, "far", 4)
    b_two = join(0.3, own_b, half_b)
    pair = join(0.6, a_next, a_prev)
    low_pair = from_low(pair, "low_pair")
    b_x1 = from_x(b_two, "x1", 1)
    b_x3 = from_x(b_two, "x3", 3)
    b_c0 = from_core(b_two, "c0")
    b_x2 = from_x(b_two, "x2", 2)
    low_own = from_low(after(own_a, low_pair), "low_own")
    low_far = from_low(a_far, "low_far")
    for_up = join(0, a_next, a_far)
    for_down = join(0, a_far, a_prev)
    up = from_z(for_up, "up", 1)
    down = from_z(for_down, "down", -1)
    b_c1 = from_core(b_x1, "c1")
    b_c2 = from_core(b_x3, "c2")
    for_low_up = join(1, (low_pair, 0, share), low_far)
    for_low_down = join(1, low_far, (low_pair, share, share))
    low_up = from_z(for_low_up, "lup", 1)
    low_down = from_z(for_low_down, "ldn", -1)
    b_c3 = from_core(b_x2, "c3")
    low_last = join(4, low_up, low_down)

    b_pieces = [b_two, b_x1, b_x3, b_x2, b_c0, b_c1, b_c2, b_c3]
    b_places = [[(dx, dhalf, dcore) for dhalf in (0, 1)] for dcore in (0, 1) for dx in (0, 1, 3, 2)]
    a_pieces = [own_a, pair, a_far, up, down, low_own, low_pair, low_far, low_last]
    a_places = [
        [(dz, dlow) for dz in steps]
        for dlow, steps in (
            (0, (0,)), (0, (1, 7)), (0, (4,)), (0, (2, 5)), (0, (3, 6)),
            (1, (0,)), (1, (1, 7)), (1, (4,)), (1, (2, 5, 3, 6)),
        )
    ]

    upper_full, upper_tile = pl.pallas_call(
        functools.partial(upper_kernel, b_places),
        out_shape=[
            jax.ShapeDtypeStruct((nb, cols), jnp.bfloat16),
            jax.ShapeDtypeStruct(row_block.shape, jnp.bfloat16),
        ],
        in_specs=[VMEM] * (len(b_pieces) + 1),
        out_specs=[VMEM, HBM],
        scratch_shapes=[pltpu.VMEM((nb, cols), jnp.bfloat16), pltpu.SemaphoreType.DMA],
        compiler_params=pltpu.CompilerParams(vmem_limit_bytes=8 << 20),
        cost_estimate=pl.CostEstimate(flops=0, bytes_accessed=0, transcendentals=0),
    )(*b_pieces, lower_inv)

    lower_tile, updated = pl.pallas_call(
        functools.partial(update_kernel, a_places),
        out_shape=[
            jax.ShapeDtypeStruct((share, rows), jnp.bfloat16),
            jax.ShapeDtypeStruct((rows, cols), jnp.float32),
        ],
        in_specs=[VMEM] * (len(a_places) + 3),
        out_specs=[HBM, HBM],
        scratch_shapes=[
            pltpu.VMEM((nb, rows), jnp.bfloat16),
            pltpu.VMEM((nb, rows), jnp.bfloat16),
            pltpu.VMEM((rows, cols), jnp.float32),
            pltpu.SemaphoreType.DMA,
            pltpu.SemaphoreType.DMA((cols // BLOCK,)),
        ],
        compiler_params=pltpu.CompilerParams(vmem_limit_bytes=12 << 20),
        cost_estimate=pl.CostEstimate(flops=2 * rows * nb * (nb + cols), bytes_accessed=0, transcendentals=0),
    )(*a_pieces, upper_inv, upper_full, trailing)
    return lower_tile.T, upper_tile, updated


def solution(mesh):
    in_specs = (P("row", "col"), P("row", "col"), P("row", "col"), P(), P())
    out_specs = (P("row", "col"), P("row", "col"), P("row", "col"))
    return jax.shard_map(
        on_device, mesh=mesh, in_specs=in_specs, out_specs=out_specs, check_vma=False
    )
```

```python
import functools

import jax
import jax.numpy as jnp
from jax import lax
from jax.experimental import pallas as pl
from jax.experimental.pallas import tpu as pltpu
from jax.sharding import PartitionSpec as P

VMEM = pl.BlockSpec(memory_space=pltpu.VMEM)
HBM = pl.BlockSpec(memory_space=pltpu.HBM)
FIRST = (((0,), (0,)), ((), ()))
BLOCK = 256


def split(row, col):
    return row >> 3, (row >> 1) & 3, row & 1, col >> 1, col & 1


def pairs_of(rows, cols, target):
    pairs = []
    for row in range(rows):
        for col in range(cols):
            half, x, core, z, low = target(*split(row, col))
            to_row = ((half % 2) * 4 + x % 4) * 2 + core
            to_col = (z % 8) * 2 + low
            pairs.append((row * cols + col, to_row * cols + to_col))
    return pairs


def place():
    return split(lax.axis_index("row"), lax.axis_index("col"))


def put(full_ref, at, piece_ref, index, share):
    rows = pl.ds(pl.multiple_of(at * share, share), share)
    full_ref[rows, :] = piece_ref[index * share : (index + 1) * share, :]


def upper_kernel(places, *refs):
    *piece_refs, lower_ref, full_ref, tile_ref, b_ref, sem = refs
    half, x, core, _, _ = place()
    share = tile_ref.shape[0]
    for ref, shards in zip(piece_refs, places, strict=True):
        for index, (dx, dhalf, dcore) in enumerate(shards):
            at = ((half ^ dhalf) * 4 + lax.rem(x + dx, 4)) * 2 + (core ^ dcore)
            put(b_ref, at, ref, index, share)
    for i in range(full_ref.shape[0] // BLOCK):
        rows, known = slice(i * BLOCK, (i + 1) * BLOCK), (i + 1) * BLOCK
        full_ref[rows, :] = jnp.dot(
            lower_ref[rows, :known], b_ref[:known, :], preferred_element_type=jnp.float32
        ).astype(full_ref.dtype)
    own = pl.ds(pl.multiple_of(lax.axis_index("row") * share, share), share)
    copy = pltpu.make_async_copy(full_ref.at[own, :], tile_ref, sem)
    copy.start()
    copy.wait()


def update_kernel(places, *refs):
    *piece_refs, upper_inv_ref, upper_ref, trailing_ref = refs[: len(places) + 3]
    tile_ref, updated_ref, a_ref, lower_ref, out_ref, tile_sem, out_sems = refs[len(places) + 3 :]
    _, _, _, z, low = place()
    share = tile_ref.shape[0]
    for ref, shards in zip(piece_refs, places, strict=True):
        for index, (dz, dlow) in enumerate(shards):
            put(a_ref, lax.rem(z + dz, 8) * 2 + (low ^ dlow), ref, index, share)
    blocks = upper_ref.shape[1] // BLOCK
    for j in range(blocks):
        cols, known = slice(j * BLOCK, (j + 1) * BLOCK), (j + 1) * BLOCK
        lower_ref[cols, :] = lax.dot_general(
            upper_inv_ref[:known, cols], a_ref[:known, :], FIRST, preferred_element_type=jnp.float32
        ).astype(lower_ref.dtype)
    own = pl.ds(pl.multiple_of(lax.axis_index("col") * share, share), share)
    tile_copy = pltpu.make_async_copy(lower_ref.at[own, :], tile_ref, tile_sem)
    tile_copy.start()
    copies = []
    for j in range(blocks):
        cols = slice(j * BLOCK, (j + 1) * BLOCK)
        out_ref[:, cols] = trailing_ref[:, cols] - lax.dot_general(
            lower_ref[...], upper_ref[:, cols], FIRST, preferred_element_type=jnp.float32
        )
        copies.append(
            pltpu.make_async_copy(out_ref.at[:, cols], updated_ref.at[:, cols], out_sems.at[j])
        )
        copies[-1].start()
    tile_copy.wait()
    for copy in copies:
        copy.wait()


def join_kernel(pieces, *refs):
    whole_ref, at = refs[-1], 0
    for ref, (start, size) in zip(refs, pieces):
        whole_ref[at : at + size, :] = ref[start : start + size, :]
        at += size


def join(time, *blocks):
    blocks = [b if isinstance(b, tuple) else (b, 0, b.shape[0]) for b in blocks]
    pieces = [b[1:] for b in blocks]
    return pl.pallas_call(
        functools.partial(join_kernel, pieces),
        out_shape=jax.ShapeDtypeStruct((sum(p[1] for p in pieces), blocks[0][0].shape[1]), jnp.bfloat16),
        in_specs=[VMEM] * len(blocks),
        out_specs=VMEM,
        compiler_params=pltpu.CompilerParams(vmem_limit_bytes=2 << 20),
        cost_estimate=pl.CostEstimate(flops=int(time * 1e9), bytes_accessed=0, transcendentals=0),
    )(*[b[0] for b in blocks])


def on_device(trailing, column_block, row_block, lower_inv, upper_inv):
    def send(block, name, target):
        with jax.named_scope(name):
            return lax.ppermute(block, ("row", "col"), pairs_of(16, 16, target))

    def from_z(block, name, step):
        return send(block, name, lambda half, x, core, z, low: (half, x, core, z - step, low))

    def from_z_by_core(block, name, step):
        return send(
            block, name, lambda half, x, core, z, low: (half, x, core, z - (step, -step)[core], low)
        )

    def from_x(block, name, step):
        return send(block, name, lambda half, x, core, z, low: (half, x - step, core, z, low))

    def from_x_by_core(block, name, step):
        return send(
            block, name, lambda half, x, core, z, low: (half, x - (step, -step)[core], core, z, low)
        )

    def from_half(block, name):
        return send(block, name, lambda half, x, core, z, low: (half ^ 1, x, core, z, low))

    def from_low(block, name):
        return send(block, name, lambda half, x, core, z, low: (half, x, core, z, low ^ 1))

    def from_core(block, name):
        return send(block, name, lambda half, x, core, z, low: (half, x, core ^ 1, z, low))

    def after(block, *others):
        return lax.optimization_barrier((block, *others))[0] if others else block

    rows, cols = trailing.shape
    nb = upper_inv.shape[0]
    share = column_block.shape[1]
    own_a, own_b = column_block.T, row_block

    half_b = from_half(own_b, "half")
    a_next = from_z(own_a, "next", 1)
    a_prev = from_z(own_a, "prev", -1)
    a_far = from_z(own_a, "far", 4)
    b_two = join(0.3, own_b, half_b)
    pair = join(0.6, a_next, a_prev)
    low_pair = from_low(pair, "low_pair")
    b_x1 = from_x(b_two, "x1", 1)
    b_x3 = from_x(b_two, "x3", 3)
    b_c0 = from_core(b_two, "c0")
    b_x2 = from_x(b_two, "x2", 2)
    low_far = from_low(a_far, "low_far")
    for_up = join(0, a_next, a_far)
    for_down = join(0, a_far, a_prev)
    up = from_z(for_up, "up", 1)
    down = from_z(for_down, "down", -1)
    b_c1 = from_core(b_x1, "c1")
    b_c2 = from_core(b_x3, "c2")
    low_own = from_low(after(own_a, b_c1, b_c2), "low_own")
    for_low_up = join(1, (low_pair, 0, share), low_far)
    for_low_down = join(1, low_far, (low_pair, share, share))
    low_up = from_z(for_low_up, "lup", 1)
    low_down = from_z(for_low_down, "ldn", -1)
    b_c3 = from_core(b_x2, "c3")
    low_last = join(4, low_up, low_down)

    b_pieces = [b_two, b_x1, b_x3, b_x2, b_c0, b_c1, b_c2, b_c3]
    b_places = [[(dx, dhalf, dcore) for dhalf in (0, 1)] for dcore in (0, 1) for dx in (0, 1, 3, 2)]
    a_pieces = [own_a, pair, a_far, up, down, low_own, low_pair, low_far, low_last]
    a_places = [
        [(dz, dlow) for dz in steps]
        for dlow, steps in (
            (0, (0,)), (0, (1, 7)), (0, (4,)), (0, (2, 5)), (0, (3, 6)),
            (1, (0,)), (1, (1, 7)), (1, (4,)), (1, (2, 5, 3, 6)),
        )
    ]

    upper_full, upper_tile = pl.pallas_call(
        functools.partial(upper_kernel, b_places),
        out_shape=[
            jax.ShapeDtypeStruct((nb, cols), jnp.bfloat16),
            jax.ShapeDtypeStruct(row_block.shape, jnp.bfloat16),
        ],
        in_specs=[VMEM] * (len(b_pieces) + 1),
        out_specs=[VMEM, HBM],
        scratch_shapes=[pltpu.VMEM((nb, cols), jnp.bfloat16), pltpu.SemaphoreType.DMA],
        compiler_params=pltpu.CompilerParams(vmem_limit_bytes=8 << 20),
        cost_estimate=pl.CostEstimate(flops=0, bytes_accessed=0, transcendentals=0),
    )(*b_pieces, lower_inv)

    lower_tile, updated = pl.pallas_call(
        functools.partial(update_kernel, a_places),
        out_shape=[
            jax.ShapeDtypeStruct((share, rows), jnp.bfloat16),
            jax.ShapeDtypeStruct((rows, cols), jnp.float32),
        ],
        in_specs=[VMEM] * (len(a_places) + 3),
        out_specs=[HBM, HBM],
        scratch_shapes=[
            pltpu.VMEM((nb, rows), jnp.bfloat16),
            pltpu.VMEM((nb, rows), jnp.bfloat16),
            pltpu.VMEM((rows, cols), jnp.float32),
            pltpu.SemaphoreType.DMA,
            pltpu.SemaphoreType.DMA((cols // BLOCK,)),
        ],
        compiler_params=pltpu.CompilerParams(vmem_limit_bytes=12 << 20),
        cost_estimate=pl.CostEstimate(flops=2 * rows * nb * (nb + cols), bytes_accessed=0, transcendentals=0),
    )(*a_pieces, upper_inv, upper_full, trailing)
    return lower_tile.T, upper_tile, updated


def solution(mesh):
    in_specs = (P("row", "col"), P("row", "col"), P("row", "col"), P(), P())
    out_specs = (P("row", "col"), P("row", "col"), P("row", "col"))
    return jax.shard_map(
        on_device, mesh=mesh, in_specs=in_specs, out_specs=out_specs, check_vma=False
    )
```

```python
import functools

import jax
import jax.numpy as jnp
from jax import lax
from jax.experimental import pallas as pl
from jax.experimental.pallas import tpu as pltpu
from jax.sharding import PartitionSpec as P

VMEM = pl.BlockSpec(memory_space=pltpu.VMEM)
HBM = pl.BlockSpec(memory_space=pltpu.HBM)
FIRST = (((0,), (0,)), ((), ()))
BLOCK = 256


def split(row, col):
    return row >> 3, (row >> 1) & 3, row & 1, col >> 1, col & 1


def pairs_of(rows, cols, target):
    pairs = []
    for row in range(rows):
        for col in range(cols):
            half, x, core, z, low = target(*split(row, col))
            to_row = ((half % 2) * 4 + x % 4) * 2 + core
            to_col = (z % 8) * 2 + low
            pairs.append((row * cols + col, to_row * cols + to_col))
    return pairs


def place():
    return split(lax.axis_index("row"), lax.axis_index("col"))


def put(full_ref, at, piece_ref, index, share):
    rows = pl.ds(pl.multiple_of(at * share, share), share)
    full_ref[rows, :] = piece_ref[index * share : (index + 1) * share, :]


def upper_kernel(places, *refs):
    *piece_refs, lower_ref, full_ref, tile_ref, b_ref, sem = refs
    half, x, core, _, _ = place()
    share = tile_ref.shape[0]
    for ref, shards in zip(piece_refs, places, strict=True):
        for index, (dx, dhalf, dcore) in enumerate(shards):
            at = ((half ^ dhalf) * 4 + lax.rem(x + dx, 4)) * 2 + (core ^ dcore)
            put(b_ref, at, ref, index, share)
    for i in range(full_ref.shape[0] // BLOCK):
        rows, known = slice(i * BLOCK, (i + 1) * BLOCK), (i + 1) * BLOCK
        full_ref[rows, :] = jnp.dot(
            lower_ref[rows, :known], b_ref[:known, :], preferred_element_type=jnp.float32
        ).astype(full_ref.dtype)
    own = pl.ds(pl.multiple_of(lax.axis_index("row") * share, share), share)
    copy = pltpu.make_async_copy(full_ref.at[own, :], tile_ref, sem)
    copy.start()
    copy.wait()


def update_kernel(places, *refs):
    *piece_refs, upper_inv_ref, upper_ref, trailing_ref = refs[: len(places) + 3]
    tile_ref, updated_ref, a_ref, lower_ref, out_ref, tile_sem, out_sems = refs[len(places) + 3 :]
    _, _, _, z, low = place()
    share = tile_ref.shape[0]
    for ref, shards in zip(piece_refs, places, strict=True):
        for index, (dz, dlow) in enumerate(shards):
            put(a_ref, lax.rem(z + dz, 8) * 2 + (low ^ dlow), ref, index, share)
    blocks = upper_ref.shape[1] // BLOCK
    for j in range(blocks):
        cols, known = slice(j * BLOCK, (j + 1) * BLOCK), (j + 1) * BLOCK
        lower_ref[cols, :] = lax.dot_general(
            upper_inv_ref[:known, cols], a_ref[:known, :], FIRST, preferred_element_type=jnp.float32
        ).astype(lower_ref.dtype)
    own = pl.ds(pl.multiple_of(lax.axis_index("col") * share, share), share)
    tile_copy = pltpu.make_async_copy(lower_ref.at[own, :], tile_ref, tile_sem)
    tile_copy.start()
    copies = []
    for j in range(blocks):
        cols = slice(j * BLOCK, (j + 1) * BLOCK)
        out_ref[:, cols] = trailing_ref[:, cols] - lax.dot_general(
            lower_ref[...], upper_ref[:, cols], FIRST, preferred_element_type=jnp.float32
        )
        copies.append(
            pltpu.make_async_copy(out_ref.at[:, cols], updated_ref.at[:, cols], out_sems.at[j])
        )
        copies[-1].start()
    tile_copy.wait()
    for copy in copies:
        copy.wait()


def join_kernel(pieces, *refs):
    whole_ref, at = refs[-1], 0
    for ref, (start, size) in zip(refs, pieces):
        whole_ref[at : at + size, :] = ref[start : start + size, :]
        at += size


def join(time, *blocks):
    blocks = [b if isinstance(b, tuple) else (b, 0, b.shape[0]) for b in blocks]
    pieces = [b[1:] for b in blocks]
    return pl.pallas_call(
        functools.partial(join_kernel, pieces),
        out_shape=jax.ShapeDtypeStruct((sum(p[1] for p in pieces), blocks[0][0].shape[1]), jnp.bfloat16),
        in_specs=[VMEM] * len(blocks),
        out_specs=VMEM,
        compiler_params=pltpu.CompilerParams(vmem_limit_bytes=2 << 20),
        cost_estimate=pl.CostEstimate(flops=int(time * 1e9), bytes_accessed=0, transcendentals=0),
    )(*[b[0] for b in blocks])


def on_device(trailing, column_block, row_block, lower_inv, upper_inv):
    def send(block, name, target):
        with jax.named_scope(name):
            return lax.ppermute(block, ("row", "col"), pairs_of(16, 16, target))

    def from_z(block, name, step):
        return send(block, name, lambda half, x, core, z, low: (half, x, core, z - step, low))

    def from_z_by_core(block, name, step):
        return send(
            block, name, lambda half, x, core, z, low: (half, x, core, z - (step, -step)[core], low)
        )

    def from_x(block, name, step):
        return send(block, name, lambda half, x, core, z, low: (half, x - step, core, z, low))

    def from_x_by_core(block, name, step):
        return send(
            block, name, lambda half, x, core, z, low: (half, x - (step, -step)[core], core, z, low)
        )

    def from_half(block, name):
        return send(block, name, lambda half, x, core, z, low: (half ^ 1, x, core, z, low))

    def from_low(block, name):
        return send(block, name, lambda half, x, core, z, low: (half, x, core, z, low ^ 1))

    def from_core(block, name):
        return send(block, name, lambda half, x, core, z, low: (half, x, core ^ 1, z, low))

    def after(block, *others):
        return lax.optimization_barrier((block, *others))[0] if others else block

    rows, cols = trailing.shape
    nb = upper_inv.shape[0]
    share = column_block.shape[1]
    own_a, own_b = column_block.T, row_block

    half_b = from_half(own_b, "half")
    a_next = from_z(own_a, "next", 1)
    a_prev = from_z(own_a, "prev", -1)
    a_far = from_z(own_a, "far", 4)
    b_two = join(0.3, own_b, half_b)
    pair = join(0.6, a_next, a_prev)
    low_pair = from_low(pair, "low_pair")
    b_x1 = from_x(b_two, "x1", 1)
    b_x3 = from_x(b_two, "x3", 3)
    b_x2 = from_x(b_two, "x2", 2)
    low_far = from_low(a_far, "low_far")
    for_up = join(0, a_next, a_far)
    for_down = join(0, a_far, a_prev)
    up = from_z(for_up, "up", 1)
    down = from_z(for_down, "down", -1)
    b_c1 = from_core(b_x1, "c1")
    b_c2 = from_core(b_x3, "c2")
    b_c0 = from_core(after(b_two, b_c1, b_c2), "c0")
    low_own = from_low(after(own_a, b_c1, b_c2), "low_own")
    for_low_up = join(1, (low_pair, 0, share), low_far)
    for_low_down = join(1, low_far, (low_pair, share, share))
    low_up = from_z(for_low_up, "lup", 1)
    low_down = from_z(for_low_down, "ldn", -1)
    b_c3 = from_core(b_x2, "c3")
    low_last = join(4, low_up, low_down)

    b_pieces = [b_two, b_x1, b_x3, b_x2, b_c0, b_c1, b_c2, b_c3]
    b_places = [[(dx, dhalf, dcore) for dhalf in (0, 1)] for dcore in (0, 1) for dx in (0, 1, 3, 2)]
    a_pieces = [own_a, pair, a_far, up, down, low_own, low_pair, low_far, low_last]
    a_places = [
        [(dz, dlow) for dz in steps]
        for dlow, steps in (
            (0, (0,)), (0, (1, 7)), (0, (4,)), (0, (2, 5)), (0, (3, 6)),
            (1, (0,)), (1, (1, 7)), (1, (4,)), (1, (2, 5, 3, 6)),
        )
    ]

    upper_full, upper_tile = pl.pallas_call(
        functools.partial(upper_kernel, b_places),
        out_shape=[
            jax.ShapeDtypeStruct((nb, cols), jnp.bfloat16),
            jax.ShapeDtypeStruct(row_block.shape, jnp.bfloat16),
        ],
        in_specs=[VMEM] * (len(b_pieces) + 1),
        out_specs=[VMEM, HBM],
        scratch_shapes=[pltpu.VMEM((nb, cols), jnp.bfloat16), pltpu.SemaphoreType.DMA],
        compiler_params=pltpu.CompilerParams(vmem_limit_bytes=8 << 20),
        cost_estimate=pl.CostEstimate(flops=0, bytes_accessed=0, transcendentals=0),
    )(*b_pieces, lower_inv)

    lower_tile, updated = pl.pallas_call(
        functools.partial(update_kernel, a_places),
        out_shape=[
            jax.ShapeDtypeStruct((share, rows), jnp.bfloat16),
            jax.ShapeDtypeStruct((rows, cols), jnp.float32),
        ],
        in_specs=[VMEM] * (len(a_places) + 3),
        out_specs=[HBM, HBM],
        scratch_shapes=[
            pltpu.VMEM((nb, rows), jnp.bfloat16),
            pltpu.VMEM((nb, rows), jnp.bfloat16),
            pltpu.VMEM((rows, cols), jnp.float32),
            pltpu.SemaphoreType.DMA,
            pltpu.SemaphoreType.DMA((cols // BLOCK,)),
        ],
        compiler_params=pltpu.CompilerParams(vmem_limit_bytes=12 << 20),
        cost_estimate=pl.CostEstimate(flops=2 * rows * nb * (nb + cols), bytes_accessed=0, transcendentals=0),
    )(*a_pieces, upper_inv, upper_full, trailing)
    return lower_tile.T, upper_tile, updated


def solution(mesh):
    in_specs = (P("row", "col"), P("row", "col"), P("row", "col"), P(), P())
    out_specs = (P("row", "col"), P("row", "col"), P("row", "col"))
    return jax.shard_map(
        on_device, mesh=mesh, in_specs=in_specs, out_specs=out_specs, check_vma=False
    )
```
